32 devices in a mesh: tok: 4 (over y, x), blk: 2 (over core), rep: 4 (over z).
Axes of the slice: x: 2, y: 2, z: 4, core: 2. Of those that a mesh axis runs over, the one named last changes fastest.
Arguments:
- block_input: bfloat16 [8448, 2048], P(('tok', 'blk', 'rep')), may hold values from -6 to 6
- cotangent: bfloat16 [8448, 2048], P(('tok', 'blk', 'rep')), may hold values from -6 to 6
- segment_ids: int32 [8448], P('tok'), may hold values from 0 to 2, as said below
- norm_gain: float32 [2048], replicated, may hold values from 0.5 to 1.5
- mlp_gain: float32 [2048], replicated, may hold values from 0.5 to 1.5
- w_input: bfloat16 [2048, 2560], P(('tok', 'blk'), 'rep'), may hold values from -0.125 to 0.125
- w_branch: bfloat16 [2048, 2560], P(('tok', 'blk'), 'rep'), may hold values from -0.125 to 0.125
- w_output: bfloat16 [2560, 2048], P('rep', ('tok', 'blk')), may hold values from -0.3125 to 0.3125
- w_gate: bfloat16 [2048, 6144], P(('tok', 'blk'), 'rep'), may hold values from -0.125 to 0.125
- w_up: bfloat16 [2048, 6144], P(('tok', 'blk'), 'rep'), may hold values from -0.125 to 0.125
- w_down: bfloat16 [6144, 2048], P('rep', ('tok', 'blk')), may hold values from -0.109375 to 0.109375
- gate_a: bfloat16 [4, 2, 2, 160, 160], P('rep', 'blk'), may hold values from -0.5 to 0.5
- gate_i: bfloat16 [4, 2, 2, 160, 160], P('rep', 'blk'), may hold values from -0.5 to 0.5
- conv_weight: float32 [4, 4, 2, 320], P(None, 'rep', 'blk'), may hold values from -3 to 3
- conv_bias: float32 [4, 2, 320], P('rep', 'blk'), may hold values from -3 to 3
- bias_a: float32 [4, 2, 320], P('rep', 'blk'), may hold values from -3 to 3
- bias_i: float32 [4, 2, 320], P('rep', 'blk'), may hold values from -3 to 3
- decay_param: float32 [4, 2, 320], P('rep', 'blk'), may hold values from 2 to 6
Outputs:
- block_out: bfloat16 [8448, 2048], P(('tok', 'blk', 'rep'))
- input_grad: float32 [8448, 2048], P(('tok', 'blk', 'rep'))
- norm_gain_grad: float32 [2048], replicated
- mlp_gain_grad: float32 [2048], replicated
- w_input_grad: float32 [2048, 2560], P(('tok', 'blk'), 'rep')
- w_branch_grad: float32 [2048, 2560], P(('tok', 'blk'), 'rep')
- w_output_grad: float32 [2560, 2048], P('rep', ('tok', 'blk'))
- w_gate_grad: float32 [2048, 6144], P(('tok', 'blk'), 'rep')
- w_up_grad: float32 [2048, 6144], P(('tok', 'blk'), 'rep')
- w_down_grad: float32 [6144, 2048], P('rep', ('tok', 'blk'))
- gate_a_grad: float32 [4, 2, 2, 160, 160], P('rep', 'blk')
- gate_i_grad: float32 [4, 2, 2, 160, 160], P('rep', 'blk')
- conv_weight_grad: float32 [4, 4, 2, 320], P(None, 'rep', 'blk')
- conv_bias_grad: float32 [4, 2, 320], P('rep', 'blk')
- bias_a_grad: float32 [4, 2, 320], P('rep', 'blk')
- bias_i_grad: float32 [4, 2, 320], P('rep', 'blk')
- decay_param_grad: float32 [4, 2, 320], P('rep', 'blk')
The draws below stay inside these ranges and needn't reach their ends.
Inputs may be any that keep to these rules, and one draw needn't show every extreme that they name: `segment_ids`: within each aligned block of 2112 slots the ids never fall, start at 0, take every value up to 2, and the slots with id 2 are the block's tail (padding, at least one slot).
All inputs are finite; a program needn't handle non-finite values.
Results may differ from the reference program's by a relative error of at most 0.01.
Values may be sent and summed in bfloat16 or wider, within the bound.
No kernel may reach another device: no remote copies, remote signals or barrier semaphores. Data moves between devices by JAX's collectives and lax.ppermute only.
A program may use at most 256 MiB of HBM per device.

```python
import jax
import jax.numpy as jnp
from jax import lax

D = 2048
R = 2560
FF = 6144
NB = 16
CONV = 4
SEQS = 2
BW = 160
RC = 320
GBD = 2
BUCKET = 2112
TOKENS = 8448
N_BLK = 2
N_REP = 4


def draw_segment_ids(key, part):
    bucket_count = TOKENS // BUCKET
    pad_key, cut_key = jax.random.split(key)
    padding = jax.random.randint(pad_key, (bucket_count, 1), 1, BUCKET // 10 + 2)
    filled = BUCKET - padding
    share_base = filled // SEQS
    spread_cut = share_base // 8
    offsets = jax.random.randint(cut_key, (bucket_count, SEQS - 1), -spread_cut, spread_cut + 1)
    boundary = jnp.arange(1, SEQS, dtype=jnp.int32)[None, :] * share_base + offsets
    positions = jnp.arange(BUCKET, dtype=jnp.int32)
    segment = jnp.sum((positions[None, :, None] >= boundary[:, None, :]).astype(jnp.int32), axis=2)
    segment = jnp.where(positions[None, :] >= filled, SEQS, segment)
    return segment.reshape(TOKENS).astype(jnp.int32)


def shard_levels(key, shape, cuts, smallest, top_value):
    def one(dim, parts):
        steps = jax.random.uniform(jax.random.fold_in(jax.random.fold_in(key, 6), dim), (parts,), jnp.float32, smallest / len(cuts), top_value / len(cuts))
        return jnp.repeat(jnp.exp(steps), shape[dim] // parts).reshape((-1,) + (1,) * (len(shape) - dim - 1))

    level = one(*cuts[0])
    for cut in cuts[1:]:
        level = level * one(*cut)
    return level


def centred(own_key, extent, deviation, limit, shards=(), kind=jnp.bfloat16):
    loudness = shard_levels(own_key, extent, shards, -0.22, 0.18) if shards else 1.0
    entries = jax.random.normal(own_key, extent, jnp.float32) * deviation * loudness
    return jnp.minimum(jnp.maximum(entries, -limit), limit).astype(kind)


def setup_inputs(seed: int = 0) -> dict:
    seeds = jax.random.split(jax.random.key(seed), 19)
    block_input = centred(seeds[0], (TOKENS, D), 1.0, 6.0, ((0, 32),))
    cotangent = centred(seeds[1], (TOKENS, D), 1.0, 6.0, ((0, 32),))
    segment_ids = draw_segment_ids(jax.random.fold_in(seeds[18], 71), 0)
    norm_gain = jnp.clip(1.0 + 0.1 * jax.random.normal(seeds[3], (D,), jnp.float32), 0.5, 1.5)
    mlp_gain = jnp.clip(1.0 + 0.1 * jax.random.normal(seeds[4], (D,), jnp.float32), 0.5, 1.5)
    w_input = centred(seeds[5], (D, R), D ** -0.5, 0.125, ((0, 8), (1, 4)))
    w_branch = centred(seeds[6], (D, R), D ** -0.5, 0.125, ((0, 8), (1, 4)))
    w_output = centred(seeds[7], (R, D), (R // 8) ** -0.5, 0.3125, ((0, 4), (1, 8)))
    w_gate = centred(seeds[8], (D, FF), D ** -0.5, 0.125, ((0, 8), (1, 4)))
    w_up = centred(seeds[9], (D, FF), D ** -0.5, 0.125, ((0, 8), (1, 4)))
    w_down = centred(seeds[10], (FF, D), (FF // 2) ** -0.5, 0.109375, ((0, 4), (1, 8)))
    gate_a = centred(seeds[11], (N_REP, N_BLK, GBD, BW, BW), BW ** -0.5, 0.5, ((0, 4), (1, 2)))
    gate_i = centred(seeds[12], (N_REP, N_BLK, GBD, BW, BW), BW ** -0.5, 0.5, ((0, 4), (1, 2)))
    conv_weight = centred(seeds[13], (CONV, N_REP, N_BLK, RC), CONV ** -0.5, 3.0, ((1, 4), (2, 2)), jnp.float32)
    conv_bias = centred(seeds[14], (N_REP, N_BLK, RC), 0.5, 3.0, ((0, 4), (1, 2)), jnp.float32)
    bias_a = centred(seeds[15], (N_REP, N_BLK, RC), 0.5, 3.0, ((0, 4), (1, 2)), jnp.float32)
    bias_i = centred(seeds[16], (N_REP, N_BLK, RC), 0.5, 3.0, ((0, 4), (1, 2)), jnp.float32)
    decay_param = jnp.clip(2.0 + 4.0 * jax.random.uniform(seeds[17], (N_REP, N_BLK, RC), jnp.float32) ** shard_levels(seeds[17], (N_REP, N_BLK, RC), ((0, 4), (1, 2)), -0.2, 0.2), 2.0, 6.0)
    return {"block_input": block_input, "cotangent": cotangent, "segment_ids": segment_ids, "norm_gain": norm_gain, "mlp_gain": mlp_gain, "w_input": w_input, "w_branch": w_branch, "w_output": w_output, "w_gate": w_gate, "w_up": w_up, "w_down": w_down, "gate_a": gate_a, "gate_i": gate_i, "conv_weight": conv_weight, "conv_bias": conv_bias, "bias_a": bias_a, "bias_i": bias_i, "decay_param": decay_param}


epsilon = 1e-06
gate_power = 8.0

@jax.custom_vjp
def low(v):
    return lax.optimization_barrier(v.astype(jnp.bfloat16)).astype(jnp.float32)

@jax.custom_vjp
def low_back(v):
    return v

def low_keep(v):
    return (low(v), None)

def low_pass(kept, grad):
    return (grad,)

def back_keep(v):
    return (v, None)

def back_low(kept, grad):
    return (low(grad),)
low.defvjp(low_keep, low_pass)
low_back.defvjp(back_keep, back_low)

def product(left_op, right_op):
    return jnp.dot(left_op, right_op, preferred_element_type=jnp.float32, precision=lax.Precision.HIGHEST)

def normalize(values, gain_vec):
    return values * lax.rsqrt(lax.optimization_barrier(jnp.mean(values * values, axis=-1, keepdims=True)) + epsilon) * gain_vec

def same_masks(bucket_ids):
    length = bucket_ids.shape[0]
    same_list = [jnp.ones((length,), jnp.float32)]
    for lag_step in range(1, CONV):
        earlier = jnp.concatenate([jnp.full((lag_step,), -1, jnp.int32), bucket_ids[:length - lag_step].astype(jnp.int32)])
        same_list.append((earlier == bucket_ids.astype(jnp.int32)).astype(jnp.float32))
    return same_list

def convolve(values, weights, bias_vec, same_list):
    length = values.shape[0]
    summed = bias_vec + weights[0] * values
    for lag_step in range(1, len(same_list)):
        shifted = jnp.concatenate([jnp.zeros((lag_step, values.shape[1]), values.dtype), values[:length - lag_step]], axis=0)
        summed = summed + weights[lag_step] * shifted * same_list[lag_step][:, None]
    return summed

def scan_states(decays, driven):

    def advance(carried, inputs):
        rate_now, push_now = inputs
        carried = rate_now * carried + push_now
        return (carried, carried)
    _, states = lax.scan(advance, jnp.zeros((decays.shape[1],), jnp.float32), (decays, driven))
    return states

def block_rows(bucket_rows, bucket_ids, params):
    norm_gain, mlp_gain, w_input, w_branch, w_output, w_gate, w_up, w_down, gate_a, gate_i, conv_weight, conv_bias, bias_a, bias_i, decay_param = params
    same_list = same_masks(bucket_ids)
    normed1 = low(normalize(bucket_rows, norm_gain))
    mixer_in = low_back(low(product(normed1, w_input)))
    branch = low_back(product(normed1, w_branch))
    conv_out = convolve(mixer_in, conv_weight, conv_bias, same_list)
    conv_low = low(conv_out).reshape(BUCKET, NB, BW)
    mixed_a = low_back(jnp.einsum('lgi,gio->lgo', conv_low, gate_a, precision=lax.Precision.HIGHEST).reshape(BUCKET, R))
    mixed_i = low_back(jnp.einsum('lgi,gio->lgo', conv_low, gate_i, precision=lax.Precision.HIGHEST).reshape(BUCKET, R))
    gate_r = jax.nn.sigmoid(mixed_a + bias_a)
    gate_in = jax.nn.sigmoid(mixed_i + bias_i)
    log_a = -gate_power * jax.nn.softplus(-decay_param) * gate_r
    decays = jnp.exp(log_a) * same_list[1][:, None]
    driven = jnp.sqrt(-jnp.expm1(2.0 * log_a)) * gate_in * conv_out
    states = low_back(low(scan_states(decays, driven)))
    merged = low(jax.nn.gelu(branch) * states)
    residual = bucket_rows + low_back(product(merged, w_output))
    normed2 = low(normalize(residual, mlp_gain))
    gate_pre = low_back(product(normed2, w_gate))
    up_pre = low_back(product(normed2, w_up))
    hidden = low(jax.nn.gelu(gate_pre) * up_pre)
    return residual + low_back(product(hidden, w_down))

def reference(block_input, cotangent, segment_ids, norm_gain, mlp_gain, w_input, w_branch, w_output, w_gate, w_up, w_down, gate_a, gate_i, conv_weight, conv_bias, bias_a, bias_i, decay_param):
    floats = tuple((element.astype(jnp.float32) for element in (block_input, norm_gain, mlp_gain, w_input, w_branch, w_output, w_gate, w_up, w_down, gate_a, gate_i, conv_weight, conv_bias, bias_a, bias_i, decay_param)))

    def forward(inputs, *params):
        shaped = (params[0], params[1], params[2], params[3], params[4], params[5], params[6], params[7], params[8].reshape(NB, BW, BW), params[9].reshape(NB, BW, BW), params[10].reshape(CONV, R), params[11].reshape(R), params[12].reshape(R), params[13].reshape(R), params[14].reshape(R))

        def one_bucket(bucket_pair):
            return block_rows(bucket_pair[0], bucket_pair[1], shaped)
        outputs = lax.map(jax.checkpoint(one_bucket), (inputs.reshape(TOKENS // BUCKET, BUCKET, D), segment_ids.reshape(TOKENS // BUCKET, BUCKET)))
        return outputs.reshape(TOKENS, D)
    block_out, pull_back = jax.vjp(forward, *floats)
    valid_rows = (segment_ids < SEQS).astype(jnp.float32)
    gradients = pull_back(cotangent.astype(jnp.float32) * valid_rows[:, None])
    return (block_out.astype(jnp.bfloat16), gradients[0], gradients[1], gradients[2], gradients[3], gradients[4], gradients[5], gradients[6], gradients[7], gradients[8], gradients[9], gradients[10], gradients[11], gradients[12], gradients[13], gradients[14], gradients[15])
```

```python
import jax
import jax.numpy as jnp
from jax import lax
from jax.experimental import pallas as pl
from jax.experimental.pallas import tpu as pltpu
from jax.sharding import PartitionSpec as P

SEQS = 2

epsilon = 1e-06
gate_power = 8.0
LANES = 128
SLAB = 8
STEP = 16
VMEM_BYTES = 56 * 1024 * 1024

f32 = jnp.float32
bf16 = jnp.bfloat16


def dot(left_op, right_op):
    return jnp.dot(left_op, right_op, preferred_element_type=f32)


def times_transposed(left_op, right_op):
    return lax.dot_general(left_op, right_op, (((1,), (1,)), ((), ())), preferred_element_type=f32)


def transposed_times(left_op, right_op):
    return lax.dot_general(left_op, right_op, (((0,), (0,)), ((), ())), preferred_element_type=f32)


def swap(values, axis, mask):
    size = lax.axis_size(axis)
    return lax.ppermute(values, axis, [(i, i ^ mask) for i in range(size)])


def in_order(first_is_mine, mine, other, axis):
    return jnp.concatenate(
        [jnp.where(first_is_mine, mine, other), jnp.where(first_is_mine, other, mine)], axis=axis
    )


def cut(values, start, size, axis=0):
    return lax.slice_in_dim(values, start, start + size, axis=axis)


def block_order(tok):
    if tok == 4:
        return [(0, 0), (0, 1), (1, 0), (3, 0), (2, 1), (3, 1), (1, 1), (2, 0)]
    return [(j, h) for j in range(tok) for h in range(2)]


def flip_blocks(blocks, tok):
    index = lax.axis_index("tok")
    bit = 1
    while bit < tok:
        flipped = (index & bit) != 0
        blocks = [jnp.where(flipped, blocks[k ^ (2 * bit)], blocks[k]) for k in range(len(blocks))]
        bit *= 2
    return blocks


def to_own_order(values):
    tok = lax.axis_size("tok")
    width = values.shape[-1] // (2 * tok)
    blocks = [cut(values, k * width, width, values.ndim - 1) for k in range(2 * tok)]
    blocks = flip_blocks(blocks, tok)
    return jnp.concatenate([blocks[2 * j + h] for j, h in block_order(tok)], axis=-1)


def from_own_order(values):
    tok = lax.axis_size("tok")
    width = values.shape[-1] // (2 * tok)
    blocks = [None] * (2 * tok)
    for place, (j, h) in enumerate(block_order(tok)):
        blocks[2 * j + h] = cut(values, place * width, width, values.ndim - 1)
    return jnp.concatenate(flip_blocks(blocks, tok), axis=-1)


def gather_pieces(piece, axis):
    tok = lax.axis_size("tok")
    if tok != 4:
        return [piece] + [swap(piece, "tok", j) for j in range(1, tok)]
    half = piece.shape[axis] // 2
    from_x = swap(piece, "tok", 1)
    from_y = swap(piece, "tok", 2)
    far_a = swap(cut(from_x, 0, half, axis), "tok", 2)
    far_b = swap(cut(from_y, half, half, axis), "tok", 1)
    return [
        piece,
        cut(from_x, 0, half, axis),
        far_a,
        cut(from_y, half, half, axis),
        far_b,
        cut(from_x, half, half, axis),
        cut(from_y, 0, half, axis),
    ]


def scatter_pieces(make, extent, axis):
    tok = lax.axis_size("tok")
    if tok != 4:
        size = extent // tok
        total = make(0, size)
        for j in range(1, tok):
            total = total + swap(make(j * size, size).astype(bf16), "tok", j).astype(f32)
        return total
    w = extent // 8
    from_x = swap(make(2 * w, 2 * w).astype(bf16), "tok", 1)
    from_y = swap(make(4 * w, 2 * w).astype(bf16), "tok", 2)
    rest = make(6 * w, 2 * w)
    own = make(0, 2 * w)
    onward_x = cut(rest, 0, w, axis) + cut(from_y, w, w, axis).astype(f32)
    onward_y = cut(rest, w, w, axis) + cut(from_x, w, w, axis).astype(f32)
    last_b = swap(onward_x.astype(bf16), "tok", 1).astype(f32)
    last_a = swap(onward_y.astype(bf16), "tok", 2).astype(f32)
    return own + jnp.concatenate(
        [cut(from_x, 0, w, axis).astype(f32) + last_a, cut(from_y, 0, w, axis).astype(f32) + last_b],
        axis=axis,
    )


def gather_rows(values):
    core = lax.axis_index("blk")
    low = (lax.axis_index("rep") & 1) == 0
    half = in_order(low, values, swap(values, "rep", 1), 0)
    return in_order(core == 0, half, swap(half, "blk", 1), 0)


def reduce_rows(make, rows):
    core = lax.axis_index("blk")
    low = lax.axis_index("rep") & 1
    other = make((1 - core) * (2 * rows), 2 * rows).astype(bf16)
    from_core = swap(other, "blk", 1)
    mine = make(core * (2 * rows), 2 * rows) + from_core.astype(f32)
    send = lax.dynamic_slice_in_dim(mine, (1 - low) * rows, rows).astype(bf16)
    keep = lax.dynamic_slice_in_dim(mine, low * rows, rows)
    return keep + swap(send, "rep", 1).astype(f32)


def row_range(values):
    return lambda start, size: lax.dynamic_slice_in_dim(values, start, size)


def normalize(values, gain_vec):
    inverse = lax.rsqrt(jnp.mean(values * values, axis=-1, keepdims=True) + epsilon)
    scaled = values * inverse
    return (scaled * gain_vec, scaled, inverse)


def normalize_back(grad_in, gain_vec, scaled, inverse):
    weighted = grad_in * gain_vec
    through = inverse * (weighted - scaled * jnp.mean(weighted * scaled, axis=-1, keepdims=True))
    return (through, jnp.sum(grad_in * scaled, axis=0))


def row_iota():
    return lax.broadcasted_iota(jnp.int32, (SLAB, LANES), 0)


def since_start(info, run, row):
    slot = row_iota() + (info[2 + run] + row)
    begin = jnp.where(slot >= info[1], info[1], jnp.where(slot >= info[0], info[0], 0))
    return slot - begin


def down(before, now, k):
    return jnp.where(row_iota() < k, pltpu.roll(before, k, 0), pltpu.roll(now, k, 0))


def up(now, after, k):
    return jnp.where(row_iota() < SLAB - k, pltpu.roll(now, SLAB - k, 0), pltpu.roll(after, SLAB - k, 0))


def last_row(values):
    return jnp.broadcast_to(values[SLAB - 1 : SLAB, :], (SLAB, LANES))


def first_row(values):
    return jnp.broadcast_to(values[0:1, :], (SLAB, LANES))


def scan_slab(rates, pushes, reverse):
    for d in (1, 2, 4):
        shift = SLAB - d if reverse else d
        mask = row_iota() < SLAB - d if reverse else row_iota() >= d
        far_rate = pltpu.roll(rates, shift, 0)
        far_push = pltpu.roll(pushes, shift, 0)
        pushes = jnp.where(mask, rates * far_push + pushes, pushes)
        rates = jnp.where(mask, rates * far_rate, rates)
    return rates, pushes


def chunks(channels):
    return [pl.ds(c * LANES, LANES) for c in range(channels // LANES)]


def row(params_ref, index, c):
    return params_ref[index : index + 1, c]


def forward_kernel(run_rows, info, x_ref, halo_ref, gates_ref, params_ref,
                   conv_ref, low_ref, r_ref, g_ref, a_ref, local_ref, reach_ref, ends_ref, mixed_ref):
    rows, channels = x_ref.shape
    steps = run_rows // STEP

    for run in range(2):
        base = run * run_rows

        def conv_step(i, before, base=base, run=run):
            at = pl.multiple_of(base + i * STEP, STEP)
            far = [since_start(info, run, i * STEP + s * SLAB) for s in range(2)]
            after = []
            for n, c in enumerate(chunks(channels)):
                x = x_ref[pl.ds(at, STEP), c].astype(f32)
                prev = before[n]
                outs = []
                for s in range(2):
                    now = x[s * SLAB : (s + 1) * SLAB]
                    total = row(params_ref, 4, c) + row(params_ref, 0, c) * now
                    for k in (1, 2, 3):
                        total = total + row(params_ref, k, c) * jnp.where(far[s] >= k, down(prev, now, k), 0.0)
                    outs.append(total)
                    prev = now
                both = jnp.concatenate(outs, axis=0)
                conv_ref[pl.ds(at, STEP), c] = both
                low_ref[pl.ds(at, STEP), c] = both.astype(bf16)
                after.append(prev)
            return tuple(after)

        first = tuple(halo_ref[run, :, c] for c in chunks(channels))
        lax.fori_loop(0, steps, conv_step, first)

    tile = rows // 6
    def gate_step(i, _):
        at = pl.multiple_of(i * tile, STEP)
        mixed_ref[pl.ds(at, tile), :] = jnp.dot(low_ref[pl.ds(at, tile), :], gates_ref[...], preferred_element_type=f32)
        return 0
    lax.fori_loop(0, 6, gate_step, 0)

    for run in range(2):
        base = run * run_rows

        def scan_step(i, carried, base=base, run=run):
            at = pl.multiple_of(base + i * STEP, STEP)
            far = [since_start(info, run, i * STEP + s * SLAB) for s in range(2)]
            after = []
            for n, c in enumerate(chunks(channels)):
                state, reach = carried[n]
                second = pl.ds(channels + n * LANES, LANES)
                for s in range(2):
                    here = pl.ds(pl.multiple_of(at + s * SLAB, SLAB), SLAB)
                    r = jax.nn.sigmoid(mixed_ref[here, c] + row(params_ref, 5, c))
                    g = jax.nn.sigmoid(mixed_ref[here, second] + row(params_ref, 6, c))
                    log_a = row(params_ref, 7, c) * r
                    e = jnp.exp(log_a)
                    power = jnp.maximum(-jnp.tanh(log_a) * (1.0 + e * e), 0.0)
                    a = jnp.where(far[s] >= 1, e, 0.0)
                    r_ref[here, c] = r
                    g_ref[here, c] = g
                    a_ref[here, c] = a
                    rates, pushes = scan_slab(a, jnp.sqrt(power) * g * conv_ref[here, c], False)
                    local_ref[here, c] = pushes + rates * state
                    reach_ref[here, c] = rates * reach
                    state = last_row(pushes) + last_row(rates) * state
                    reach = last_row(rates) * reach
                after.append((state, reach))
            return tuple(after)

        zero = tuple((jnp.zeros((SLAB, LANES), f32), jnp.ones((SLAB, LANES), f32)) for _ in chunks(channels))
        done = lax.fori_loop(0, steps, scan_step, zero)
        for n, c in enumerate(chunks(channels)):
            ends_ref[run, :, c] = done[n][0]
            ends_ref[2 + run, :, c] = done[n][1]


def backward_scan_kernel(run_rows, a_ref, grad_ref, part_ref, reach_ref, ends_ref):
    channels = a_ref.shape[1]
    steps = run_rows // STEP
    for run in range(2):
        base = run * run_rows

        def step(j, carried, base=base):
            at = pl.multiple_of(base + (steps - 1 - j) * STEP, STEP)
            after = []
            for n, c in enumerate(chunks(channels)):
                flow, reach = carried[n]
                grads = grad_ref[pl.ds(at, STEP), c].astype(f32)
                for s in (1, 0):
                    here = pl.ds(pl.multiple_of(at + s * SLAB, SLAB), SLAB)
                    grad = grads[s * SLAB : (s + 1) * SLAB]
                    a = a_ref[here, c]
                    rates, pushes = scan_slab(a, a * grad, True)
                    flows = pushes + rates * flow
                    reaches = rates * reach
                    part_ref[here, c] = grad + up(flows, flow, 1)
                    reach_ref[here, c] = up(reaches, reach, 1)
                    flow = first_row(pushes) + first_row(rates) * flow
                    reach = first_row(rates) * reach
                after.append((flow, reach))
            return tuple(after)

        zero = tuple((jnp.zeros((SLAB, LANES), f32), jnp.ones((SLAB, LANES), f32)) for _ in chunks(channels))
        done = lax.fori_loop(0, steps, step, zero)
        for n, c in enumerate(chunks(channels)):
            ends_ref[run, :, c] = done[n][0]


def backward_kernel(run_rows, info, part_ref, reach_ref, flow_ref, states_ref, enter_ref, r_ref, g_ref, conv_ref,
                    gates_ref, params_ref, mixed_ref, conv_grad_ref, sums_ref):
    rows, channels = r_ref.shape
    steps = run_rows // STEP
    sums_ref[...] = jnp.zeros(sums_ref.shape, f32)
    for run in range(2):
        base = run * run_rows

        def step(i, carried, base=base, run=run):
            at = pl.multiple_of(base + i * STEP, STEP)
            far = [since_start(info, run, i * STEP + s * SLAB) for s in range(2)]
            after = []
            for n, c in enumerate(chunks(channels)):
                prev, sum_a, sum_i, sum_d = carried[n]
                second = pl.ds(channels + n * LANES, LANES)
                flow = flow_ref[run, :, c]
                grads_a, grads_i = [], []
                for s in range(2):
                    here = pl.ds(pl.multiple_of(at + s * SLAB, SLAB), SLAB)
                    total = part_ref[here, c] + reach_ref[here, c] * flow
                    states = states_ref[here, c]
                    r, g, conv = r_ref[here, c], g_ref[here, c], conv_ref[here, c]
                    log_a = row(params_ref, 7, c) * r
                    e = jnp.exp(log_a)
                    power = jnp.maximum(-jnp.tanh(log_a) * (1.0 + e * e), 0.0)
                    inverse = lax.rsqrt(power)
                    root = power * inverse
                    a = jnp.where(far[s] >= 1, e, 0.0)
                    through = total * g
                    grad_log = total * down(prev, states, 1) * a - through * conv * (e * e) * inverse
                    grad_a = grad_log * row(params_ref, 7, c) * r * (1.0 - r)
                    direct = through * root
                    grad_i = direct * conv * (1.0 - g)
                    conv_grad_ref[here, c] = direct
                    sum_a = sum_a + grad_a
                    sum_i = sum_i + grad_i
                    sum_d = sum_d + grad_log * r
                    grads_a.append(grad_a)
                    grads_i.append(grad_i)
                    prev = states
                mixed_ref[pl.ds(at, STEP), c] = jnp.concatenate(grads_a, axis=0).astype(bf16)
                mixed_ref[pl.ds(at, STEP), second] = jnp.concatenate(grads_i, axis=0).astype(bf16)
                after.append((prev, sum_a, sum_i, sum_d))
            return tuple(after)

        nothing = jnp.zeros((SLAB, LANES), f32)
        first = tuple((enter_ref[run, :, c], nothing, nothing, nothing) for c in chunks(channels))
        done = lax.fori_loop(0, steps, step, first)
        for n, c in enumerate(chunks(channels)):
            for k in range(3):
                sums_ref[k : k + 1, c] += jnp.sum(done[n][1 + k], axis=0, keepdims=True)

    tile = rows // 6
    def gate_step(i, _):
        at = pl.multiple_of(i * tile, STEP)
        conv_grad_ref[pl.ds(at, tile), :] += times_transposed(mixed_ref[pl.ds(at, tile), :], gates_ref[...])
        return 0
    lax.fori_loop(0, 6, gate_step, 0)


def conv_back_kernel(run_rows, info, conv_grad_ref, halo_ref, x_ref, params_ref, grad_ref, sums_ref):
    rows, channels = x_ref.shape
    steps = run_rows // STEP
    sums_ref[...] = jnp.zeros(sums_ref.shape, f32)
    for run in range(2):
        base = run * run_rows

        def step(j, carried, base=base, run=run):
            i = steps - 1 - j
            at = pl.multiple_of(base + i * STEP, STEP)
            far = [since_start(info, run, i * STEP + s * SLAB) for s in range(3)]
            after = []
            for n, c in enumerate(chunks(channels)):
                later, totals = carried[n]
                totals = list(totals)
                x = x_ref[pl.ds(at, STEP), c].astype(f32)
                outs = [None, None]
                for s in (1, 0):
                    now = conv_grad_ref[pl.ds(pl.multiple_of(at + s * SLAB, SLAB), SLAB), c]
                    here = x[s * SLAB : (s + 1) * SLAB]
                    out = row(params_ref, 0, c) * now
                    totals[0] = totals[0] + now * here
                    for k in (1, 2, 3):
                        moved = up(jnp.where(far[s] >= k, now, 0.0), jnp.where(far[s + 1] >= k, later, 0.0), k)
                        out = out + row(params_ref, k, c) * moved
                        totals[k] = totals[k] + moved * here
                    totals[4] = totals[4] + now
                    outs[s] = out
                    later = now
                grad_ref[pl.ds(at, STEP), c] = jnp.concatenate(outs, axis=0).astype(bf16)
                after.append((later, tuple(totals)))
            return tuple(after)

        nothing = jnp.zeros((SLAB, LANES), f32)
        first = tuple((halo_ref[run, :, c], (nothing,) * 5) for c in chunks(channels))
        done = lax.fori_loop(0, steps, step, first)
        for n, c in enumerate(chunks(channels)):
            for k in range(5):
                sums_ref[k : k + 1, c] += jnp.sum(done[n][1][k], axis=0, keepdims=True)


def call_kernel(kernel, inputs, outputs, flops=0, scratch=(), scalars=True):
    vmem = pl.BlockSpec(memory_space=pltpu.VMEM)
    smem = pl.BlockSpec(memory_space=pltpu.SMEM)
    specs = [smem if scalars and k == 0 else vmem for k in range(len(inputs))]
    moved = sum(v.size * v.dtype.itemsize for v in inputs) + sum(
        o[0][0] * o[0][1] * jnp.dtype(o[1]).itemsize for o in outputs
    )
    return pl.pallas_call(
        kernel,
        in_specs=specs,
        out_specs=[vmem] * len(outputs),
        out_shape=[jax.ShapeDtypeStruct(s, d) for s, d in outputs],
        scratch_shapes=list(scratch),
        compiler_params=pltpu.CompilerParams(vmem_limit_bytes=VMEM_BYTES),
        cost_estimate=pl.CostEstimate(flops=flops, bytes_accessed=moved, transcendentals=0),
    )(*inputs)


def body(
    block_input,
    cotangent,
    segment_ids,
    norm_gain,
    mlp_gain,
    w_input,
    w_branch,
    w_output,
    w_gate,
    w_up,
    w_down,
    gate_a,
    gate_i,
    conv_weight,
    conv_bias,
    bias_a,
    bias_i,
    decay_param,
):
    rows, width = block_input.shape
    bucket = segment_ids.shape[0]
    core = lax.axis_index("blk")
    rep = lax.axis_index("rep")
    first_core = core == 0
    early = (rep & 2) == 0

    run_rows = 2 * rows
    group_rows = 2 * run_rows
    taps = conv_weight.shape[0]
    own_channels = conv_weight.shape[-1]
    channels = 2 * own_channels
    blocks = gate_a.shape[2]
    block_width = gate_a.shape[3]
    own_hidden = w_gate.shape[1] // 2
    hidden_count = 2 * own_hidden

    start1 = jnp.sum((segment_ids < 1).astype(jnp.int32))
    start2 = jnp.sum((segment_ids < 2).astype(jnp.int32))
    run_base = (rep // 2) * run_rows
    info = jnp.stack([start1, start2, run_base, run_base + bucket // 2]).astype(jnp.int32)
    own_slot = core * (bucket // 2) + rep * rows + jnp.arange(rows, dtype=jnp.int32)
    valid = (own_slot < start2).astype(f32)[:, None]

    gain1 = to_own_order(norm_gain[None, :])
    gain2 = to_own_order(mlp_gain[None, :])

    x_first = to_own_order(block_input).astype(f32)
    normed1, scaled1, inverse1 = normalize(x_first, gain1)
    rows1 = gather_rows(normed1.astype(bf16))

    def split_columns(values):
        half = values.shape[1] // 2
        low, high = values[:, :half], values[:, half:]
        return jnp.where(first_core, low, high), jnp.where(first_core, high, low)

    def split_rows(values):
        half = values.shape[0] // 2
        low, high = values[:half], values[half:]
        return jnp.where(first_core, low, high), jnp.where(first_core, high, low)

    def row_weights(one, two):
        one_mine, one_other = split_columns(one)
        two_mine, two_other = split_columns(two)
        mine = jnp.concatenate([one_mine, two_mine], axis=1)
        came = swap(jnp.concatenate([one_other, two_other], axis=1), "blk", 1)
        own = in_order(first_core, mine, came, 0)
        far = swap(own, "rep", 2)
        n = one_mine.shape[1]
        piece = jnp.concatenate([own[:, :n], far[:, :n], own[:, n:], far[:, n:]], axis=1)
        pieces = gather_pieces(piece, 0)
        return (
            jnp.concatenate([p[:, : 2 * n] for p in pieces], axis=0),
            jnp.concatenate([p[:, 2 * n :] for p in pieces], axis=0),
        )

    def column_weights(values):
        mine, other = split_rows(values)
        came = swap(other, "blk", 1)
        own = in_order(first_core, mine, came, 1)
        piece = jnp.concatenate([own, swap(own, "rep", 2)], axis=0)
        return jnp.concatenate(gather_pieces(piece, 1), axis=1)

    full_in, full_branch = row_weights(w_input, w_branch)

    small = jnp.concatenate(
        [
            conv_weight.reshape(taps, own_channels),
            conv_bias.reshape(1, own_channels),
            bias_a.reshape(1, own_channels),
            bias_i.reshape(1, own_channels),
            decay_param.reshape(1, own_channels),
        ],
        axis=0,
    )
    small = jnp.concatenate([small, swap(small, "rep", 2)], axis=1)
    decay_row = small[taps + 3 :]
    params = jnp.concatenate([small[: taps + 3], -gate_power * jax.nn.softplus(-decay_row)], axis=0)
    gates = jnp.stack(
        [gate_a.reshape(blocks, block_width, block_width), gate_i.reshape(blocks, block_width, block_width)]
    )
    gates = jnp.concatenate([gates, swap(gates, "rep", 2)], axis=1)

    def spread_gate(gate):
        strips = []
        for k in range(2 * blocks):
            left = jnp.zeros((block_width, k * block_width), bf16)
            right = jnp.zeros((block_width, (2 * blocks - 1 - k) * block_width), bf16)
            strips.append(jnp.concatenate([left, gate[k], right], axis=1))
        return jnp.concatenate(strips, axis=0)

    gate_matrix = jnp.concatenate([spread_gate(gates[0]), spread_gate(gates[1])], axis=1)

    def from_far(values):
        came = swap(values, "rep", 2)
        return jnp.concatenate([came[..., own_channels:], came[..., :own_channels]], axis=-1)

    mixer_in = dot(rows1, full_in).astype(bf16)
    branch = dot(rows1, full_branch)
    tails = jnp.stack([mixer_in[run_rows - SLAB : run_rows], mixer_in[group_rows - SLAB :]])
    tails = from_far(tails).astype(f32)
    halo = jnp.stack([tails[0], jnp.where(early, tails[0], tails[1])])
    full = (group_rows, channels)
    conv_out, conv_low, gate_r, gate_in, decays, local, reach, ends = call_kernel(
        lambda *refs: forward_kernel(run_rows, *refs),
        (info, mixer_in, halo, gate_matrix, params),
        ((full, f32), (full, bf16), (full, f32), (full, f32), (full, f32), (full, f32), (full, f32),
         ((4, SLAB, channels), f32)),
        flops=4 * group_rows * channels * channels,
        scratch=(pltpu.VMEM((group_rows, 2 * channels), f32),),
    )
    own_end = ends[:, 0]
    far_end = from_far(own_end)
    h0, h1, p0, p1 = own_end[0], own_end[1], own_end[2], own_end[3]
    fh0, fh1, fp0, fp1 = far_end[0], far_end[1], far_end[2], far_end[3]
    enter0 = jnp.where(early, jnp.zeros_like(fh0), fh0)
    enter1 = jnp.where(early, fh0 + fp0 * h0, fh1 + fp1 * (h0 + p0 * fh0))
    enter = jnp.stack([enter0, enter1])
    states = (
        local.reshape(2, run_rows, channels) + reach.reshape(2, run_rows, channels) * enter[:, None, :]
    ).reshape(full)
    states_low = states.astype(bf16).astype(f32)
    activated = jax.nn.gelu(branch)
    merged = (activated * states_low).astype(bf16)

    full_out = column_weights(w_output)
    take_merged = row_range(merged)
    residual = x_first + reduce_rows(lambda s, n: dot(take_merged(s, n), full_out), rows)

    normed2, scaled2, inverse2 = normalize(residual, gain2)
    rows2 = gather_rows(normed2.astype(bf16))
    full_gate, full_up = row_weights(w_gate, w_up)
    gate_pre = dot(rows2, full_gate)
    up_pre = dot(rows2, full_up)
    gate_act, gate_back = jax.vjp(jax.nn.gelu, gate_pre)
    hidden = (gate_act * up_pre).astype(bf16)
    full_down = column_weights(w_down)

    grad_final = to_own_order(cotangent).astype(f32) * valid
    final_grad_rows = gather_rows(grad_final.astype(bf16))
    grad_hidden = times_transposed(final_grad_rows, full_down)
    grad_gate = gate_back(grad_hidden * up_pre)[0].astype(bf16)
    grad_up = (grad_hidden * gate_act).astype(bf16)
    take_gate, take_up = row_range(grad_gate), row_range(grad_up)
    grad_normed2 = reduce_rows(
        lambda s, n: times_transposed(take_gate(s, n), full_gate) + times_transposed(take_up(s, n), full_up), rows
    )
    through2, gain2_term = normalize_back(grad_normed2, gain2, scaled2, inverse2)
    grad_residual = grad_final + through2
    residual_rows = gather_rows(grad_residual.astype(bf16))

    take_hidden = row_range(hidden)
    final_rows = residual + reduce_rows(lambda s, n: dot(take_hidden(s, n), full_down), rows)
    block_out = from_own_order(final_rows.astype(bf16))

    def own_columns(values, axis):
        half = values.shape[axis] // 2
        return [cut(values, k * half, half, axis) for k in range(2)]

    def finish_rows(total, n):
        far = jnp.concatenate([total[:, n : 2 * n], total[:, 3 * n :]], axis=1).astype(bf16)
        own = jnp.concatenate([total[:, :n], total[:, 2 * n : 3 * n]], axis=1) + swap(far, "rep", 2).astype(f32)
        low, high = own_columns(own, 0)
        mine = jnp.where(first_core, low, high)
        came = swap(jnp.where(first_core, high, low), "blk", 1)
        return tuple(in_order(first_core, cut(mine, k * n, n, 1), cut(came, k * n, n, 1), 1) for k in range(2))

    def finish_columns(total):
        n = total.shape[0] // 2
        own = total[:n] + swap(total[n:].astype(bf16), "rep", 2).astype(f32)
        low, high = own_columns(own, 1)
        mine = jnp.where(first_core, low, high)
        came = swap(jnp.where(first_core, high, low), "blk", 1)
        return in_order(first_core, mine, came, 0)

    down_total = scatter_pieces(
        lambda s, n: transposed_times(hidden, cut(final_grad_rows, s, n, 1)), width, 1
    )
    grad_down_w = finish_columns(down_total)
    both_grads = jnp.concatenate([grad_gate, grad_up], axis=1)
    mlp_total = scatter_pieces(lambda s, n: transposed_times(cut(rows2, s, n, 1), both_grads), width, 0)
    grad_gate_w, grad_up_w = finish_rows(mlp_total, own_hidden)

    grad_merged = times_transposed(residual_rows, full_out)
    _, branch_back = jax.vjp(jax.nn.gelu, branch)
    grad_branch = branch_back(grad_merged * states_low)[0].astype(bf16)
    grad_states = (grad_merged * activated).astype(bf16)
    part, back_reach, flows = call_kernel(
        lambda *refs: backward_scan_kernel(run_rows, *refs),
        (decays, grad_states),
        ((full, f32), (full, f32), ((2, SLAB, channels), f32)),
        scalars=False,
    )
    own_flow = flows[:, 0]
    far_flow = from_far(own_flow)
    u0, u1 = own_flow[0], own_flow[1]
    fu0, fu1 = far_flow[0], far_flow[1]
    flow1 = jnp.where(early, fu1, jnp.zeros_like(fu1))
    flow0 = jnp.where(early, fu0 + fp0 * (u1 + p1 * fu1), fu1 + fp1 * u1)

    def wide(values):
        return jnp.broadcast_to(values[:, None, :], (2, SLAB, channels))

    grad_mixed, grad_conv, sums = call_kernel(
        lambda *refs: backward_kernel(run_rows, *refs),
        (info, part, back_reach, wide(jnp.stack([flow0, flow1])), states, wide(enter), gate_r, gate_in, conv_out,
         gate_matrix, params),
        (((group_rows, 2 * channels), bf16), (full, f32), ((SLAB, channels), f32)),
        flops=4 * group_rows * channels * channels,
    )
    heads = from_far(jnp.stack([grad_conv[:SLAB], grad_conv[run_rows : run_rows + SLAB]]))
    after = jnp.stack(
        [jnp.where(early, heads[0], heads[1]), jnp.where(early, heads[1], jnp.zeros_like(heads[1]))]
    )
    grad_mixer_in, conv_sums = call_kernel(
        lambda *refs: conv_back_kernel(run_rows, *refs),
        (info, grad_conv, after, mixer_in, params),
        ((full, bf16), ((SLAB, channels), f32)),
    )
    take_in, take_branch = row_range(grad_mixer_in), row_range(grad_branch)
    grad_normed1 = reduce_rows(
        lambda s, n: times_transposed(take_in(s, n), full_in) + times_transposed(take_branch(s, n), full_branch),
        rows,
    )
    through1, gain1_term = normalize_back(grad_normed1, gain1, scaled1, inverse1)
    input_grad = from_own_order(grad_residual + through1)

    out_total = scatter_pieces(
        lambda s, n: transposed_times(merged, cut(residual_rows, s, n, 1)), width, 1
    )
    grad_out_w = finish_columns(out_total)
    mixer_grads = jnp.concatenate([grad_mixer_in, grad_branch], axis=1)
    mixer_total = scatter_pieces(lambda s, n: transposed_times(cut(rows1, s, n, 1), mixer_grads), width, 0)
    grad_in_w, grad_branch_w = finish_rows(mixer_total, own_channels)

    def sum_over(values, axis):
        size = lax.axis_size(axis)
        bit = 1
        while bit < size:
            values = values + swap(values, axis, bit)
            bit *= 2
        return values

    gate_grads = transposed_times(conv_low, grad_mixed)

    def gate_block(which, k):
        at = k * block_width
        return gate_grads[at : at + block_width, which * channels + at : which * channels + at + block_width]

    own_gates = jnp.stack([jnp.stack([gate_block(w, k) for k in range(blocks)]) for w in range(2)])
    far_gates = jnp.stack([jnp.stack([gate_block(w, k) for k in range(blocks, 2 * blocks)]) for w in range(2)])
    gate_sum = sum_over(own_gates + swap(far_gates, "rep", 2), "tok")
    decay_grad = sums[2:3] * (gate_power * jax.nn.sigmoid(-decay_row))
    small_grads = jnp.concatenate([conv_sums[: taps + 1], sums[:2], decay_grad], axis=0)
    small_sum = sum_over(small_grads[:, :own_channels] + swap(small_grads[:, own_channels:], "rep", 2), "tok")

    gain_terms = from_own_order(jnp.stack([gain1_term, gain2_term]))
    gain_sum = sum_over(sum_over(sum_over(gain_terms, "blk"), "rep"), "tok")

    return (
        block_out,
        input_grad,
        gain_sum[0],
        gain_sum[1],
        grad_in_w,
        grad_branch_w,
        grad_out_w,
        grad_gate_w,
        grad_up_w,
        grad_down_w,
        gate_sum[0].reshape(gate_a.shape),
        gate_sum[1].reshape(gate_i.shape),
        small_sum[:taps].reshape(conv_weight.shape),
        small_sum[taps].reshape(conv_bias.shape),
        small_sum[taps + 1].reshape(bias_a.shape),
        small_sum[taps + 2].reshape(bias_i.shape),
        small_sum[taps + 3].reshape(decay_param.shape),
    )


def solution(mesh):
    rows_spec = P(("tok", "blk", "rep"), None)
    by_rows = P(("tok", "blk"), "rep")
    by_columns = P("rep", ("tok", "blk"))
    channel = P("rep", "blk", None)
    gate_spec = P("rep", "blk", None, None, None)
    taps_spec = P(None, "rep", "blk", None)
    return jax.shard_map(
        body,
        mesh=mesh,
        in_specs=(
            rows_spec, rows_spec, P("tok"), P(), P(),
            by_rows, by_rows, by_columns, by_rows, by_rows, by_columns,
            gate_spec, gate_spec, taps_spec, channel, channel, channel, channel,
        ),
        out_specs=(
            rows_spec, rows_spec, P(), P(),
            by_rows, by_rows, by_columns, by_rows, by_rows, by_columns,
            gate_spec, gate_spec, taps_spec, channel, channel, channel, channel,
        ),
        check_vma=False,
    )
```
